128 devices in a mesh: occ: 4 (over y), vir: 32 (over z, x, core).
Axes of the slice: x: 4, y: 4, z: 4, core: 2. Of those that a mesh axis runs over, the one named last changes fastest.
Arguments:
- amplitudes: bfloat16 [32, 32, 589824], P(None, None, ('occ', 'vir')), may hold values from -6 to 6
- ladder_integrals: bfloat16 [32, 32, 589824], P(None, None, ('occ', 'vir')), may hold values from -0.015625 to 0.015625
- driver: float32 [32, 32, 1024], P('occ', 'vir'), may hold values from -6 to 6
- occ_energy: float32 [32], replicated, may hold values from -2 to -0.5
- vir_energy: float32 [32], replicated, may hold values from 0.5 to 4
- occ_irrep: int32 [32], replicated, may hold values from 0 to 3
- vir_tile_irrep: int32 [12], replicated, may hold values from 0 to 3
Outputs:
- updated: float32 [32, 32, 1024], P('occ', 'vir')
The draws below stay inside these ranges and needn't reach their ends.
All inputs are finite; a program needn't handle non-finite values.
Results may differ from the reference program's by a relative error of at most 0.0003.
Values sent between devices are 32-bit elements; how exact they have to be, the bound alone decides.
A program may use at most 128 MiB of HBM per device.

```python
import jax
import jax.numpy as jnp
from jax import lax

NV = 768
TILE = 64
NO_W = 32
NA = 32
N_OCC = 4
N_VIR = 32


def touch_ends(values, stream_key, low, high):
    longest = values.shape.index(max(values.shape))
    spots = []
    for shift in (0, 1):
        where = [jax.random.randint(jax.random.fold_in(stream_key, axis), (), 0, length) for axis, length in enumerate(values.shape)]
        where[longest] = (where[longest] + shift) % values.shape[longest]
        spots.append(tuple(where))
    return values.at[spots[0]].set(low).at[spots[1]].set(high)


def raised(values, own_key, source, target, blocks, factor):
    owner, partner = [(jnp.arange(values.shape[dim]) // (values.shape[dim] // blocks)).reshape([-1 if axis == dim else 1 for axis in range(values.ndim)]) for dim in (source, target)]
    chosen = jax.random.permutation(own_key, blocks)[partner]
    strong = (owner == chosen) | (owner == (partner + blocks // 2) % blocks)
    return jnp.where(strong, factor * values, values)


def shard_levels(stream_key, dims, pieces, smallest, top_value):
    def one(dim, shards_of):
        steps = jax.random.uniform(jax.random.fold_in(jax.random.fold_in(stream_key, 6), dim), (shards_of,), jnp.float32, smallest / len(pieces), top_value / len(pieces))
        return jnp.repeat(jnp.exp(steps), dims[dim] // shards_of).reshape((-1,) + (1,) * (len(dims) - dim - 1))

    factor_of = one(*pieces[0])
    for cut in pieces[1:]:
        factor_of = factor_of * one(*cut)
    return factor_of


def scatter_about(own_key, extent, deviation, most, cuts=(), held_as=jnp.bfloat16):
    entries = jax.random.normal(own_key, extent, jnp.float32) * deviation
    if len(cuts) > 0:
        entries = shard_levels(own_key, extent, cuts, -0.22, 0.18) * entries
    return jnp.clip(entries, min=-most, max=most).astype(held_as)


def noise_with(stream_key, extent, width, reach, split, heavy, kind=jnp.bfloat16):
    drawn = width * jax.random.normal(stream_key, extent, jnp.float32)
    if split:
        drawn = drawn * shard_levels(stream_key, extent, split, -0.22, 0.18)
    return jnp.clip(raised(drawn, jax.random.fold_in(stream_key, 3), *heavy), -reach, reach).astype(kind)


def setup_inputs(seed: int = 0) -> dict:
    arg_keys = jax.random.split(jax.random.key(seed), 8)
    amplitudes = scatter_about(arg_keys[0], (NO_W, NO_W, NV * NV), 1.0, 6.0, ((2, 128),))
    ladder_integrals = noise_with(arg_keys[1], (NA, NA, NV * NV), (NV * NV) ** -0.5, 0.015625, ((2, 128),), (2, 0, 32, 2.75))
    driver = scatter_about(arg_keys[2], (NO_W, NA, NO_W * NA), 1.0, 6.0, ((0, 4), (1, 32)), jnp.float32)
    occ_energy = jnp.clip(jax.random.uniform(arg_keys[3], (NO_W,), jnp.float32, -2.0, -0.5), -2.0, -0.5)
    vir_energy = jnp.clip(jax.random.uniform(arg_keys[4], (NA,), jnp.float32, 0.5, 4.0), 0.5, 4.0)
    occ_irrep = touch_ends(jax.random.randint(arg_keys[5], (NO_W,), 0, 4), jax.random.fold_in(arg_keys[5], 1), 0, 3).astype(jnp.int32)
    vir_tile_irrep = touch_ends(jax.random.randint(arg_keys[6], (NV // TILE,), 0, 4), jax.random.fold_in(arg_keys[6], 1), 0, 3).astype(jnp.int32)
    return {"amplitudes": amplitudes, "ladder_integrals": ladder_integrals, "driver": driver, "occ_energy": occ_energy, "vir_energy": vir_energy, "occ_irrep": occ_irrep, "vir_tile_irrep": vir_tile_irrep}


def cd_labels(positions, labels):
    tiles = jnp.arange(labels.shape[0], dtype=jnp.int32)
    first = (positions // NV) // TILE
    second = (positions % NV) // TILE
    lab_first = jnp.sum(jnp.where(first[:, None] == tiles[None, :], labels[None, :], 0), axis=1)
    lab_second = jnp.sum(jnp.where(second[:, None] == tiles[None, :], labels[None, :], 0), axis=1)
    return jnp.bitwise_xor(lab_first, lab_second).astype(jnp.int32)


def reference(amplitudes, ladder_integrals, driver, occ_energy, vir_energy, occ_irrep, vir_tile_irrep):
    total_cd = NV * NV
    blocks = N_OCC * N_VIR
    block_width = total_cd // blocks
    pair_label = jnp.bitwise_xor(occ_irrep[:, None], occ_irrep[None, :]).reshape(-1)
    amp_rows = amplitudes.reshape(NO_W * NO_W, total_cd)
    int_rows = ladder_integrals.reshape(NA * NA, total_cd)

    def step(block, acc):
        start = (block * block_width).astype(jnp.int32)
        positions = start + jnp.arange(block_width, dtype=jnp.int32)
        labels = cd_labels(positions, vir_tile_irrep)
        keep = jnp.bitwise_xor(pair_label[:, None], labels[None, :]) == 0
        amp_block = lax.dynamic_slice_in_dim(amp_rows, start, block_width, 1)
        masked = jnp.where(keep, amp_block, jnp.zeros_like(amp_block))
        int_block = lax.dynamic_slice_in_dim(int_rows, start, block_width, 1)
        return acc + jnp.dot(masked, int_block.T, preferred_element_type=jnp.float32)

    acc = lax.fori_loop(0, blocks, step, jnp.zeros((NO_W * NO_W, NA * NA), jnp.float32))
    ladder = acc.reshape(NO_W, NO_W, NA, NA)
    paired = ladder + ladder.transpose(1, 0, 3, 2)
    ordered = paired.transpose(0, 2, 1, 3)
    denom = (occ_energy[:, None, None, None] + occ_energy[None, None, :, None]
             - vir_energy[None, :, None, None] - vir_energy[None, None, None, :])
    result = (driver.reshape(NO_W, NA, NO_W, NA) + ordered) / denom
    return result.reshape(NO_W, NA, NO_W * NA)
```

```python
import jax
import jax.numpy as jnp
from jax import lax
from jax.experimental import pallas as pl
from jax.experimental.pallas import tpu as pltpu
from jax.sharding import PartitionSpec as P

NV = 768
TILE = 64
K = 4608
KC = 1536
MESH = pl.DeviceIdType.MESH

ORDERS = ("yzx", "zxy", "xyz", "yzx", "zxy", "xyz", "zxy", "yzx")


def kernel(
    v_hbm, a_hbm, drv_hbm, occ_e, vir_e, occ_l, tile_l, out_ref,
    v, a, lab, own, oth, rc, r1, x1, r2, x2, r3, t2, ts, rm, zt, wt, drv,
    vsem, asem, dsem, csend, crecv, s1, q1, s2, q2, s3, q3, msend, mrecv,
):
    y = lax.axis_index("occ")
    w = lax.axis_index("vir")
    z, x, c = w // 8, (w // 2) % 4, w % 2
    oc = 1 - c
    me = {"y": y, "z": z, "x": x}

    def peer(axis, r):
        m = lax.rem(me[axis] + r, 4)
        if axis == "y":
            return m, (m, w)
        if axis == "z":
            return m, (y, m * 8 + x * 2 + c)
        return m, (y, z * 8 + m * 2 + c)

    partner = (y, z * 8 + x * 2 + oc)
    barrier = pltpu.get_barrier_semaphore()
    pl.semaphore_signal(barrier, inc=1, device_id=partner, device_id_type=MESH)
    for axis in "yzx":
        for r in (1, 2, 3):
            pl.semaphore_signal(barrier, inc=1, device_id=peer(axis, r)[1], device_id_type=MESH)

    def vcopy(half, core, kc):
        ks = pl.ds(kc * KC, KC)
        return pltpu.make_async_copy(v_hbm.at[:, core, :, ks], v.at[half, :, :, ks], vsem.at[half, kc])

    def acopy(p, kc):
        ks = pl.ds(kc * KC, KC)
        return pltpu.make_async_copy(a_hbm.at[:, p, :, :, ks], a.at[p, :, :, :, ks], asem.at[p, kc])

    for kc in range(3):
        vcopy(0, oc, kc).start()
        acopy(0, kc).start()
    for kc in range(3):
        vcopy(1, c, kc).start()
    for kc in range(3):
        acopy(1, kc).start()
    dcopy = pltpu.make_async_copy(drv_hbm, drv, dsem)
    dcopy.start()

    d_pos = lax.broadcasted_iota(jnp.int32, (8, NV), 1) // TILE
    d_lab = jnp.zeros((8, NV), jnp.int32)
    for t in range(NV // TILE):
        d_lab = jnp.where(d_pos == t, tile_l[t], d_lab)
    rank = y * 32 + w
    for cl in range(K // NV):
        c_lab = tile_l[(rank * (K // NV) + cl) // TILE]
        lab[:, pl.ds(cl * NV, NV)] = jnp.bitwise_xor(d_lab, c_lab)
    row = lax.broadcasted_iota(jnp.int32, (32, 128), 0)
    occ_col = jnp.zeros((32, 128), jnp.int32)
    for j in range(32):
        occ_col = jnp.where(row == j, occ_l[j], occ_col)
    occ_col = occ_col[:, :1].astype(jnp.float32).astype(jnp.bfloat16)

    def masked(p, k0, kt):
        parts = []
        base = lab[0:1, pl.ds(k0, kt)]
        for yy in range(4):
            for i in range(4):
                want = jnp.bitwise_xor(base, occ_l[yy * 8 + p * 4 + i])
                want = want.astype(jnp.float32).astype(jnp.bfloat16)
                blk = a[p, yy, i, :, pl.ds(k0, kt)]
                parts.append(jnp.where(occ_col == want, blk, jnp.zeros_like(blk)))
        return jnp.concatenate(parts, axis=0)

    def product(half, p, k0, kt):
        lhs = v[half, :, :, pl.ds(k0, kt)].reshape(512, kt)
        return lax.dot_general(
            lhs, masked(p, k0, kt), (((1,), (1,)), ((), ())), preferred_element_type=jnp.float32
        )

    def put(dst, p, d, add):
        for yy in range(4):
            blk = d[:, yy * 128:(yy + 1) * 128].reshape(4, 4, 4, 8, 128)
            if add:
                dst[p, yy] += blk
            else:
                dst[p, yy] = blk

    def core_copy(p):
        return pltpu.make_async_remote_copy(
            oth.at[p], rc.at[p], csend.at[p], crecv.at[p], device_id=partner, device_id_type=MESH
        )

    def at_axis(ref, lead, names, axis, m):
        idx = tuple(lead) + tuple(m if n == axis else slice(None) for n in names)
        return ref.at[idx]

    def stage_copies(s, p, g):
        h = p * 4 + g
        order = ORDERS[h]
        axis = order[s]
        out = []
        for r in (1, 2, 3):
            m, dev = peer(axis, r)
            if s == 0:
                src = own.at[tuple([p] + [m if n == axis else slice(None) for n in "yzx"] + [g])]
                dst, ss, rs = r1.at[h, r - 1], s1.at[h, r - 1], q1.at[h, r - 1]
            elif s == 1:
                names = [n for n in "yzx" if n != order[0]]
                src = x1.at[tuple([h] + [m if n == axis else slice(None) for n in names])]
                dst, ss, rs = r2.at[h, r - 1], s2.at[h, r - 1], q2.at[h, r - 1]
            else:
                src = x2.at[h, m]
                dst, ss, rs = r3.at[h, r - 1], s3.at[h, r - 1], q3.at[h, r - 1]
            out.append(pltpu.make_async_remote_copy(src, dst, ss, rs, device_id=dev, device_id_type=MESH))
        return out

    def stage_send(s, p, g):
        for cp in stage_copies(s, p, g):
            cp.start()

    def stage_recv(s, p, g):
        h = p * 4 + g
        order = ORDERS[h]
        axis = order[s]
        m = me[axis]
        for cp in stage_copies(s, p, g):
            cp.wait_recv()
        if s == 0:
            mine = own[tuple([p] + [m if n == axis else slice(None) for n in "yzx"] + [g])]
            x1[h] = mine + (r1[h, 0] + r1[h, 1] + r1[h, 2])
        elif s == 1:
            names = [n for n in "yzx" if n != order[0]]
            mine = x1[tuple([h] + [m if n == axis else slice(None) for n in names])]
            x2[h] = mine + (r2[h, 0] + r2[h, 1] + r2[h, 2])
        else:
            tot = x2[h, m] + (r3[h, 0] + r3[h, 1] + r3[h, 2])
            t2[p, g * 8:(g + 1) * 8, :] = tot
            ts[p, g * 8:(g + 1) * 8, 0, :] = tot

    for kc in range(3):
        vcopy(0, oc, kc).wait()
        acopy(0, kc).wait()
        put(oth, 0, product(0, 0, kc * KC, KC), kc > 0)
    pl.semaphore_wait(barrier, 10)
    core_copy(0).start()
    for kc in range(3):
        vcopy(1, c, kc).wait()
    put(own, 0, product(1, 0, 0, K), False)
    core_copy(0).wait_recv()
    own[0] = own[0] + rc[0]
    for g in range(4):
        stage_send(0, 0, g)
    for kc in range(3):
        acopy(1, kc).wait()
    put(oth, 1, product(0, 1, 0, K), False)
    core_copy(1).start()
    put(own, 1, product(1, 1, 0, K), False)
    core_copy(1).wait_recv()
    own[1] = own[1] + rc[1]
    for g in range(4):
        stage_send(0, 1, g)
    for p in range(2):
        for g in range(4):
            stage_recv(0, p, g)
            stage_send(1, p, g)
    for p in range(2):
        for g in range(4):
            stage_recv(1, p, g)
            stage_send(2, p, g)
    for p in range(2):
        for g in range(4):
            stage_recv(2, p, g)

    def send_row(r, carry):
        d = lax.rem(rank + r, 128)
        dy, dw = d // 32, lax.rem(d, 32)
        pltpu.make_async_remote_copy(
            ts.at[:, dw], rm.at[y, :, w], msend, mrecv, device_id=(dy, dw), device_id_type=MESH
        ).start()
        return carry

    pltpu.make_async_copy(ts.at[:, w], rm.at[y, :, w], mrecv).start()
    lax.fori_loop(1, 128, send_row, 0)

    lane = lax.broadcasted_iota(jnp.int32, (8, 128), 1)
    sub = lax.broadcasted_iota(jnp.int32, (8, 128), 0)
    for p in range(2):
        zt[p * 128:(p + 1) * 128, :] = jnp.concatenate([t2[p].T, jnp.zeros((128, 96), jnp.float32)], axis=1)
    dcopy.wait()
    occ_j = jnp.zeros((8, 128), jnp.float32)
    vir_b = jnp.zeros((8, 128), jnp.float32)
    jpos = sub * 4 + lane // 32
    bpos = lane % 32
    for k in range(32):
        occ_j = jnp.where(jpos == k, occ_e[k], occ_j)
        vir_b = jnp.where(bpos == k, vir_e[k], vir_b)
    mine = []
    for i in range(8):
        acc = zt[pl.ds(i * 32, 8, stride=4), :]
        for jj in range(1, 4):
            acc = acc + pltpu.roll(zt[pl.ds(i * 32 + jj, 8, stride=4), :], jj * 32, 1)
        mine.append(drv[i] + acc)

    pltpu.make_async_copy(rm, rm, mrecv).wait()
    for t in range(8):
        blk = rm[t // 2, t % 2, :, 0, :].T
        zt[0:128, :] = jnp.concatenate([blk, jnp.zeros((128, 96), jnp.float32)], axis=1)
        acc = zt[pl.ds(pl.multiple_of(y * 8, 8), 8), :]
        for jj in range(1, 4):
            acc = acc + pltpu.roll(zt[pl.ds(pl.multiple_of(jj * 32 + y * 8, 8), 8), :], jj * 32, 1)
        wt[t * 8:(t + 1) * 8, :] = acc
    va = vir_e[w]
    for i in range(8):
        tot = mine[i] + wt[pl.ds(i, 8, stride=8), :]
        den = (occ_e[y * 8 + i] + occ_j) - va - vir_b
        out_ref[i] = tot / den

    for p in range(2):
        core_copy(p).wait_send()
        for g in range(4):
            for s in range(3):
                for cp in stage_copies(s, p, g):
                    cp.wait_send()
    flat = rm.at[0:3]
    pltpu.make_async_copy(flat, flat, msend).wait()
    rest = rm.at[3, :, 0:31]
    pltpu.make_async_copy(rest, rest, msend).wait()


def local(amplitudes, ladder_integrals, driver, occ_energy, vir_energy, occ_irrep, vir_tile_irrep):
    f32, bf16 = jnp.float32, jnp.bfloat16
    dma = pltpu.SemaphoreType.DMA
    any_ = pl.BlockSpec(memory_space=pl.ANY)
    smem = pl.BlockSpec(memory_space=pltpu.SMEM)
    out = pl.pallas_call(
        kernel,
        out_shape=jax.ShapeDtypeStruct((8, 8, 128), f32),
        in_specs=[any_, any_, any_, smem, smem, smem, smem],
        out_specs=pl.BlockSpec(memory_space=pltpu.VMEM),
        scratch_shapes=[
            pltpu.VMEM((2, 16, 32, K), bf16),
            pltpu.VMEM((2, 4, 4, 32, K), bf16),
            pltpu.VMEM((8, K), jnp.int32),
            pltpu.VMEM((2, 4, 4, 4, 4, 8, 128), f32),
            pltpu.VMEM((2, 4, 4, 4, 4, 8, 128), f32),
            pltpu.VMEM((2, 4, 4, 4, 4, 8, 128), f32),
            pltpu.VMEM((8, 3, 4, 4, 8, 128), f32),
            pltpu.VMEM((8, 4, 4, 8, 128), f32),
            pltpu.VMEM((8, 3, 4, 8, 128), f32),
            pltpu.VMEM((8, 4, 8, 128), f32),
            pltpu.VMEM((8, 3, 8, 128), f32),
            pltpu.VMEM((2, 32, 128), f32),
            pltpu.VMEM((2, 32, 1, 128), f32),
            pltpu.VMEM((4, 2, 32, 1, 128), f32),
            pltpu.VMEM((256, 128), f32),
            pltpu.VMEM((64, 128), f32),
            pltpu.VMEM((8, 8, 128), f32),
            dma((2, 3)), dma((2, 3)), dma,
            dma((2,)), dma((2,)),
            dma((8, 3)), dma((8, 3)), dma((8, 3)), dma((8, 3)), dma((8, 3)), dma((8, 3)),
            dma, dma,
        ],
        compiler_params=pltpu.CompilerParams(
            collective_id=0, has_side_effects=True, vmem_limit_bytes=60 * 2**20
        ),
        name="ladder",
    )(
        ladder_integrals.reshape(16, 2, 32, K),
        amplitudes.reshape(4, 2, 4, 32, K),
        driver.reshape(8, 8, 128),
        occ_energy, vir_energy, occ_irrep, vir_tile_irrep,
    )
    return out.reshape(8, 1, 1024)


def solution(mesh):
    return jax.shard_map(
        local,
        mesh=mesh,
        in_specs=(
            P(None, None, ("occ", "vir")),
            P(None, None, ("occ", "vir")),
            P("occ", "vir", None),
            P(),
            P(),
            P(),
            P(),
        ),
        out_specs=P("occ", "vir", None),
        check_vma=False,
    )
```

```python
import jax
import jax.numpy as jnp
from jax import lax
from jax.experimental import pallas as pl
from jax.experimental.pallas import tpu as pltpu
from jax.sharding import PartitionSpec as P

NV = 768
TILE = 64
K = 4608
KC = 1536
MESH = pl.DeviceIdType.MESH

ORDERS = ("yzx", "zyx", "yzx", "yzx", "xzy", "zxy", "xzy", "zxy")


def kernel(
    v_hbm, a_hbm, drv_hbm, occ_e, vir_e, occ_l, tile_l, out_ref,
    v, a, lab, own, oth, rc, r1, x1, r2, x2, r3, t2, ts, rm, et, zt, wt, drv,
    vsem, asem, dsem, csend, crecv, s1, q1, s2, q2, s3, q3, msend, mrecv,
):
    y = lax.axis_index("occ")
    w = lax.axis_index("vir")
    z, x, c = w // 8, (w // 2) % 4, w % 2
    oc = 1 - c
    me = {"y": y, "z": z, "x": x}

    def peer(axis, r):
        m = lax.rem(me[axis] + r, 4)
        if axis == "y":
            return m, (m, w)
        if axis == "z":
            return m, (y, m * 8 + x * 2 + c)
        return m, (y, z * 8 + m * 2 + c)

    partner = (y, z * 8 + x * 2 + oc)
    barrier = pltpu.get_barrier_semaphore()
    pl.semaphore_signal(barrier, inc=1, device_id=partner, device_id_type=MESH)
    for axis in "yzx":
        for r in (1, 2, 3):
            pl.semaphore_signal(barrier, inc=1, device_id=peer(axis, r)[1], device_id_type=MESH)

    def vcopy(half, core, kc):
        ks = pl.ds(kc * KC, KC)
        return pltpu.make_async_copy(v_hbm.at[:, core, :, ks], v.at[half, :, :, ks], vsem.at[half, kc])

    def acopy(p, kc):
        ks = pl.ds(kc * KC, KC)
        return pltpu.make_async_copy(a_hbm.at[:, p, :, :, ks], a.at[p, :, :, :, ks], asem.at[p, kc])

    for kc in range(3):
        vcopy(0, oc, kc).start()
        acopy(0, kc).start()
    for kc in range(3):
        vcopy(1, c, kc).start()
    for kc in range(3):
        acopy(1, kc).start()
    dcopy = pltpu.make_async_copy(drv_hbm, drv, dsem)
    dcopy.start()

    d_pos = lax.broadcasted_iota(jnp.int32, (8, NV), 1) // TILE
    d_lab = jnp.zeros((8, NV), jnp.int32)
    for t in range(NV // TILE):
        d_lab = jnp.where(d_pos == t, tile_l[t], d_lab)
    rank = y * 32 + w
    for cl in range(K // NV):
        c_lab = tile_l[(rank * (K // NV) + cl) // TILE]
        lab[:, pl.ds(cl * NV, NV)] = jnp.bitwise_xor(d_lab, c_lab)
    row = lax.broadcasted_iota(jnp.int32, (32, 128), 0)
    occ_col = jnp.zeros((32, 128), jnp.int32)
    for j in range(32):
        occ_col = jnp.where(row == j, occ_l[j], occ_col)
    occ_col = occ_col[:, :1].astype(jnp.float32).astype(jnp.bfloat16)

    def masked(p, k0, kt):
        parts = []
        base = lab[0:1, pl.ds(k0, kt)]
        for yy in range(4):
            for i in range(4):
                want = jnp.bitwise_xor(base, occ_l[yy * 8 + p * 4 + i])
                want = want.astype(jnp.float32).astype(jnp.bfloat16)
                blk = a[p, yy, i, :, pl.ds(k0, kt)]
                blk = jnp.where(occ_col == want, blk, jnp.zeros_like(blk))
                a[p, yy, i, :, pl.ds(k0, kt)] = blk
                parts.append(blk)
        return jnp.concatenate(parts, axis=0)

    def unit(half, p, bh, k0, kt, dst, first, add):
        rhs = masked(p, k0, kt) if first else a[p, :, :, :, pl.ds(k0, kt)].reshape(512, kt)
        lhs = v[half, :, bh * 16:(bh + 1) * 16, pl.ds(k0, kt)].reshape(256, kt)
        d = lax.dot_general(lhs, rhs, (((1,), (1,)), ((), ())), preferred_element_type=jnp.float32)
        for yy in range(4):
            blk = d[:, yy * 128:(yy + 1) * 128].reshape(4, 4, 2, 8, 128)
            if add:
                dst[p, yy, :, :, 2 * bh:2 * bh + 2] += blk
            else:
                dst[p, yy, :, :, 2 * bh:2 * bh + 2] = blk

    def core_copy(p, bh):
        gs = pl.ds(2 * bh, 2)
        return pltpu.make_async_remote_copy(
            oth.at[p, :, :, :, gs], rc.at[p, :, :, :, gs], csend.at[2 * p + bh], crecv.at[2 * p + bh],
            device_id=partner, device_id_type=MESH,
        )

    def core_add(p, bh):
        core_copy(p, bh).wait_recv()
        gs = pl.ds(2 * bh, 2)
        own[p, :, :, :, gs] = own[p, :, :, :, gs] + rc[p, :, :, :, gs]

    def at_axis(ref, lead, names, axis, m):
        idx = tuple(lead) + tuple(m if n == axis else slice(None) for n in names)
        return ref.at[idx]

    def stage_copies(s, p, g):
        h = p * 4 + g
        order = ORDERS[h]
        axis = order[s]
        out = []
        for r in (1, 2, 3):
            m, dev = peer(axis, r)
            if s == 0:
                src = own.at[tuple([p] + [m if n == axis else slice(None) for n in "yzx"] + [g])]
                dst, ss, rs = r1.at[h, r - 1], s1.at[h, r - 1], q1.at[h, r - 1]
            elif s == 1:
                names = [n for n in "yzx" if n != order[0]]
                src = x1.at[tuple([h] + [m if n == axis else slice(None) for n in names])]
                dst, ss, rs = r2.at[h, r - 1], s2.at[h, r - 1], q2.at[h, r - 1]
            else:
                src = x2.at[h, m]
                dst, ss, rs = r3.at[h, r - 1], s3.at[h, r - 1], q3.at[h, r - 1]
            out.append(pltpu.make_async_remote_copy(src, dst, ss, rs, device_id=dev, device_id_type=MESH))
        return out

    def stage_send(s, p, g):
        for cp in stage_copies(s, p, g):
            cp.start()

    def stage_recv(s, p, g):
        h = p * 4 + g
        order = ORDERS[h]
        axis = order[s]
        m = me[axis]
        for cp in stage_copies(s, p, g):
            cp.wait_recv()
        if s == 0:
            mine = own[tuple([p] + [m if n == axis else slice(None) for n in "yzx"] + [g])]
            x1[h] = mine + (r1[h, 0] + r1[h, 1] + r1[h, 2])
        elif s == 1:
            names = [n for n in "yzx" if n != order[0]]
            mine = x1[tuple([h] + [m if n == axis else slice(None) for n in names])]
            x2[h] = mine + (r2[h, 0] + r2[h, 1] + r2[h, 2])
        else:
            tot = x2[h, m] + (r3[h, 0] + r3[h, 1] + r3[h, 2])
            t2[p, g * 8:(g + 1) * 8, :] = tot

    lane = lax.broadcasted_iota(jnp.int32, (8, 128), 1)
    sub = lax.broadcasted_iota(jnp.int32, (8, 128), 0)

    def mirror_rows(p, g):
        h = p * 4 + g
        moved = []
        for m in range(4):
            val = x2[h, m]
            out = val
            for s in (-3, -2, -1, 1, 2, 3):
                out = jnp.where((lane // 32) - (lane // 8) % 4 == s, pltpu.roll(val, (24 * s) % 128, 1), out)
            moved.append(out)
        for yy in range(4):
            out = moved[yy]
            for m in range(4):
                if m != yy:
                    out = jnp.where(lane // 32 == m, pltpu.roll(moved[m], (32 * (m - yy)) % 128, 1), out)
            ts[p, yy, g * 8:(g + 1) * 8, 0, :] = out

    red = (x, y)
    keep = (y * 8 + z * 2 + c, w)

    def mirror_send(p, bh):
        def one(k, carry):
            e = lax.rem(k + rank, 64)
            dy, dw = e // 16, bh * 16 + lax.rem(e, 16)
            src, dst = ts.at[p, dy, dw], rm.at[p, red[p], keep[p]]
            other = dy * 32 + dw != rank

            @pl.when(other)
            def _():
                pltpu.make_async_remote_copy(
                    src, dst, msend.at[p], mrecv.at[p], device_id=(dy, dw), device_id_type=MESH
                ).start()

            @pl.when(jnp.logical_not(other))
            def _():
                pltpu.make_async_copy(src, dst, mrecv.at[p]).start()

            return carry

        lax.fori_loop(0, 64, one, 0)

    def part(p, bh):
        return ((p, 2 * bh), (p, 2 * bh + 1))

    def first(p, bh):
        core_add(p, bh)
        for q in part(p, bh):
            stage_send(0, *q)

    def second(p, bh):
        for q in part(p, bh):
            stage_recv(0, *q)
            stage_send(1, *q)

    def third(p, bh):
        for q in part(p, bh):
            stage_recv(1, *q)
            stage_send(2, *q)
            mirror_rows(*q)
        mirror_send(p, bh)

    def last(p, bh):
        for q in part(p, bh):
            stage_recv(2, *q)

    for kc in range(3):
        vcopy(0, oc, kc).wait()
        acopy(0, kc).wait()
        unit(0, 0, 0, kc * KC, KC, oth, True, kc > 0)
    pl.semaphore_wait(barrier, 10)
    core_copy(0, 0).start()
    unit(0, 0, 1, 0, K, oth, False, False)
    core_copy(0, 1).start()
    for kc in range(3):
        vcopy(1, c, kc).wait()
    unit(1, 0, 0, 0, K, own, False, False)
    first(0, 0)
    for kc in range(3):
        acopy(1, kc).wait()
    unit(0, 1, 0, 0, K, oth, True, False)
    core_copy(1, 0).start()
    unit(1, 0, 1, 0, K, own, False, False)
    first(0, 1)
    unit(1, 1, 0, 0, K, own, False, False)
    first(1, 0)
    unit(0, 1, 1, 0, K, oth, False, False)
    core_copy(1, 1).start()
    second(0, 0)
    unit(1, 1, 1, 0, K, own, False, False)
    first(1, 1)
    second(0, 1)
    second(1, 0)
    third(0, 0)
    second(1, 1)
    third(0, 1)
    third(1, 0)
    third(1, 1)
    last(0, 0)
    last(0, 1)
    last(1, 0)
    last(1, 1)

    for p in range(2):
        zt[p * 128:(p + 1) * 128, :] = jnp.concatenate([t2[p].T, jnp.zeros((128, 96), jnp.float32)], axis=1)
    dcopy.wait()
    occ_j = jnp.zeros((8, 128), jnp.float32)
    vir_b = jnp.zeros((8, 128), jnp.float32)
    jpos = sub * 4 + lane // 32
    bpos = lane % 32
    for k in range(32):
        occ_j = jnp.where(jpos == k, occ_e[k], occ_j)
        vir_b = jnp.where(bpos == k, vir_e[k], vir_b)
    mine = []
    for i in range(8):
        acc = zt[pl.ds(i * 32, 8, stride=4), :]
        for jj in range(1, 4):
            acc = acc + pltpu.roll(zt[pl.ds(i * 32 + jj, 8, stride=4), :], jj * 32, 1)
        mine.append(drv[i] + acc)

    for p in range(2):
        pltpu.make_async_copy(rm.at[p], rm.at[p], mrecv.at[p]).wait()
        for k in range(32):
            row = (rm[p, 0, k] + rm[p, 1, k]) + (rm[p, 2, k] + rm[p, 3, k])
            for m in range(4):
                at = (k // 2) * 8 + m * 2 + k % 2 if p == 0 else m * 32 + k
                et[at] = row if m == 0 else pltpu.roll(row, 128 - 32 * m, 1)
        tr = et[:, 0, :].T
        for yy in range(4):
            acc = None
            for i in range(4):
                blk = tr[i * 8:(i + 1) * 8, :]
                blk = blk if i == yy else pltpu.roll(blk, (32 * (i - yy)) % 128, 1)
                acc = blk if acc is None else jnp.where(lane // 32 == i, blk, acc)
            t = yy * 2 + p
            wt[t * 8:(t + 1) * 8, :] = acc
    va = vir_e[w]
    for i in range(8):
        tot = mine[i] + wt[pl.ds(i, 8, stride=8), :]
        den = (occ_e[y * 8 + i] + occ_j) - va - vir_b
        out_ref[i] = tot / den

    for p in range(2):
        for bh in range(2):
            core_copy(p, bh).wait_send()
        for g in range(4):
            for s in range(3):
                for cp in stage_copies(s, p, g):
                    cp.wait_send()
    for p in range(2):
        for flat in (rm.at[p, 0:3], rm.at[p, 3, 0:31]):
            pltpu.make_async_copy(flat, flat, msend.at[p]).wait()


def local(amplitudes, ladder_integrals, driver, occ_energy, vir_energy, occ_irrep, vir_tile_irrep):
    f32, bf16 = jnp.float32, jnp.bfloat16
    dma = pltpu.SemaphoreType.DMA
    any_ = pl.BlockSpec(memory_space=pl.ANY)
    smem = pl.BlockSpec(memory_space=pltpu.SMEM)
    out = pl.pallas_call(
        kernel,
        out_shape=jax.ShapeDtypeStruct((8, 8, 128), f32),
        in_specs=[any_, any_, any_, smem, smem, smem, smem],
        out_specs=pl.BlockSpec(memory_space=pltpu.VMEM),
        scratch_shapes=[
            pltpu.VMEM((2, 16, 32, K), bf16),
            pltpu.VMEM((2, 4, 4, 32, K), bf16),
            pltpu.VMEM((8, K), jnp.int32),
            pltpu.VMEM((2, 4, 4, 4, 4, 8, 128), f32),
            pltpu.VMEM((2, 4, 4, 4, 4, 8, 128), f32),
            pltpu.VMEM((2, 4, 4, 4, 4, 8, 128), f32),
            pltpu.VMEM((8, 3, 4, 4, 8, 128), f32),
            pltpu.VMEM((8, 4, 4, 8, 128), f32),
            pltpu.VMEM((8, 3, 4, 8, 128), f32),
            pltpu.VMEM((8, 4, 8, 128), f32),
            pltpu.VMEM((8, 3, 8, 128), f32),
            pltpu.VMEM((2, 32, 128), f32),
            pltpu.VMEM((2, 4, 32, 1, 128), f32),
            pltpu.VMEM((2, 4, 32, 1, 128), f32),
            pltpu.VMEM((128, 1, 128), f32),
            pltpu.VMEM((256, 128), f32),
            pltpu.VMEM((64, 128), f32),
            pltpu.VMEM((8, 8, 128), f32),
            dma((2, 3)), dma((2, 3)), dma,
            dma((4,)), dma((4,)),
            dma((8, 3)), dma((8, 3)), dma((8, 3)), dma((8, 3)), dma((8, 3)), dma((8, 3)),
            dma((2,)), dma((2,)),
        ],
        compiler_params=pltpu.CompilerParams(
            collective_id=0, has_side_effects=True, vmem_limit_bytes=60 * 2**20
        ),
        name="ladder",
    )(
        ladder_integrals.reshape(16, 2, 32, K),
        amplitudes.reshape(4, 2, 4, 32, K),
        driver.reshape(8, 8, 128),
        occ_energy, vir_energy, occ_irrep, vir_tile_irrep,
    )
    return out.reshape(8, 1, 1024)


def solution(mesh):
    return jax.shard_map(
        local,
        mesh=mesh,
        in_specs=(
            P(None, None, ("occ", "vir")),
            P(None, None, ("occ", "vir")),
            P("occ", "vir", None),
            P(),
            P(),
            P(),
            P(),
        ),
        out_specs=P("occ", "vir", None),
        check_vma=False,
    )
```

```python
import jax
import jax.numpy as jnp
from jax import lax
from jax.experimental import pallas as pl
from jax.experimental.pallas import tpu as pltpu
from jax.sharding import PartitionSpec as P

NV = 768
TILE = 64
K = 4608
KC = 1536
MESH = pl.DeviceIdType.MESH

ORDERS = ("yzx", "zyx", "yzx", "yzx", "xzy", "xzy", "zxy", "xzy")


def kernel(
    v_hbm, a_hbm, drv_hbm, occ_e, vir_e, occ_l, tile_l, out_ref,
    v, a, lab, own, oth, rc, r1, x1, r2, x2, r3, t2, ts, rm, et, zt, wt, drv,
    vsem, asem, dsem, csend, crecv, s1, q1, s2, q2, s3, q3, msend, mrecv,
):
    y = lax.axis_index("occ")
    w = lax.axis_index("vir")
    z, x, c = w // 8, (w // 2) % 4, w % 2
    oc = 1 - c
    me = {"y": y, "z": z, "x": x}

    def peer(axis, r):
        m = lax.rem(me[axis] + r, 4)
        if axis == "y":
            return m, (m, w)
        if axis == "z":
            return m, (y, m * 8 + x * 2 + c)
        return m, (y, z * 8 + m * 2 + c)

    partner = (y, z * 8 + x * 2 + oc)
    barrier = pltpu.get_barrier_semaphore()
    pl.semaphore_signal(barrier, inc=1, device_id=partner, device_id_type=MESH)
    for axis in "yzx":
        for r in (1, 2, 3):
            pl.semaphore_signal(barrier, inc=1, device_id=peer(axis, r)[1], device_id_type=MESH)

    def vcopy(half, core, kc):
        ks = pl.ds(kc * KC, KC)
        return pltpu.make_async_copy(v_hbm.at[:, core, :, ks], v.at[half, :, :, ks], vsem.at[half, kc])

    def acopy(p, kc):
        ks = pl.ds(kc * KC, KC)
        return pltpu.make_async_copy(a_hbm.at[:, p, :, :, ks], a.at[p, :, :, :, ks], asem.at[p, kc])

    for kc in range(3):
        vcopy(0, oc, kc).start()
        acopy(0, kc).start()
    for kc in range(3):
        vcopy(1, c, kc).start()
    for kc in range(3):
        acopy(1, kc).start()
    dcopy = pltpu.make_async_copy(drv_hbm, drv, dsem)
    dcopy.start()

    d_pos = lax.broadcasted_iota(jnp.int32, (8, NV), 1) // TILE
    d_lab = jnp.zeros((8, NV), jnp.int32)
    for t in range(NV // TILE):
        d_lab = jnp.where(d_pos == t, tile_l[t], d_lab)
    rank = y * 32 + w
    for cl in range(K // NV):
        c_lab = tile_l[(rank * (K // NV) + cl) // TILE]
        lab[:, pl.ds(cl * NV, NV)] = jnp.bitwise_xor(d_lab, c_lab)
    row = lax.broadcasted_iota(jnp.int32, (32, 128), 0)
    occ_col = jnp.zeros((32, 128), jnp.int32)
    for j in range(32):
        occ_col = jnp.where(row == j, occ_l[j], occ_col)
    occ_col = occ_col[:, :1].astype(jnp.float32).astype(jnp.bfloat16)

    def masked(p, k0, kt):
        parts = []
        base = lab[0:1, pl.ds(k0, kt)]
        for yy in range(4):
            for i in range(4):
                want = jnp.bitwise_xor(base, occ_l[yy * 8 + p * 4 + i])
                want = want.astype(jnp.float32).astype(jnp.bfloat16)
                blk = a[p, yy, i, :, pl.ds(k0, kt)]
                blk = jnp.where(occ_col == want, blk, jnp.zeros_like(blk))
                a[p, yy, i, :, pl.ds(k0, kt)] = blk
                parts.append(blk)
        return jnp.concatenate(parts, axis=0)

    def unit(half, p, bh, k0, kt, dst, first, add):
        lo, n = (0, 32) if bh is None else (bh * 16, 16)
        rhs = masked(p, k0, kt) if first else a[p, :, :, :, pl.ds(k0, kt)].reshape(512, kt)
        lhs = v[half, :, lo:lo + n, pl.ds(k0, kt)].reshape(16 * n, kt)
        d = lax.dot_general(lhs, rhs, (((1,), (1,)), ((), ())), preferred_element_type=jnp.float32)
        gs = slice(lo // 8, (lo + n) // 8)
        for yy in range(4):
            blk = d[:, yy * 128:(yy + 1) * 128].reshape(4, 4, n // 8, 8, 128)
            if add:
                dst[p, yy, :, :, gs] += blk
            else:
                dst[p, yy, :, :, gs] = blk

    def core_copy(p, bh):
        gs = pl.ds(2 * bh, 2)
        return pltpu.make_async_remote_copy(
            oth.at[p, :, :, :, gs], rc.at[p, :, :, :, gs], csend.at[2 * p + bh], crecv.at[2 * p + bh],
            device_id=partner, device_id_type=MESH,
        )

    def core_add(p, bh):
        core_copy(p, bh).wait_recv()
        gs = pl.ds(2 * bh, 2)
        own[p, :, :, :, gs] = own[p, :, :, :, gs] + rc[p, :, :, :, gs]

    def at_axis(ref, lead, names, axis, m):
        idx = tuple(lead) + tuple(m if n == axis else slice(None) for n in names)
        return ref.at[idx]

    def stage_copies(s, p, g):
        h = p * 4 + g
        order = ORDERS[h]
        axis = order[s]
        out = []
        for r in (1, 2, 3):
            m, dev = peer(axis, r)
            if s == 0:
                src = own.at[tuple([p] + [m if n == axis else slice(None) for n in "yzx"] + [g])]
                dst, ss, rs = r1.at[h, r - 1], s1.at[h, r - 1], q1.at[h, r - 1]
            elif s == 1:
                names = [n for n in "yzx" if n != order[0]]
                src = x1.at[tuple([h] + [m if n == axis else slice(None) for n in names])]
                dst, ss, rs = r2.at[h, r - 1], s2.at[h, r - 1], q2.at[h, r - 1]
            else:
                src = x2.at[h, m]
                dst, ss, rs = r3.at[h, r - 1], s3.at[h, r - 1], q3.at[h, r - 1]
            out.append(pltpu.make_async_remote_copy(src, dst, ss, rs, device_id=dev, device_id_type=MESH))
        return out

    def stage_send(s, p, g):
        for cp in stage_copies(s, p, g):
            cp.start()

    def stage_recv(s, p, g):
        h = p * 4 + g
        order = ORDERS[h]
        axis = order[s]
        m = me[axis]
        for cp in stage_copies(s, p, g):
            cp.wait_recv()
        if s == 0:
            mine = own[tuple([p] + [m if n == axis else slice(None) for n in "yzx"] + [g])]
            x1[h] = mine + (r1[h, 0] + r1[h, 1] + r1[h, 2])
        elif s == 1:
            names = [n for n in "yzx" if n != order[0]]
            mine = x1[tuple([h] + [m if n == axis else slice(None) for n in names])]
            x2[h] = mine + (r2[h, 0] + r2[h, 1] + r2[h, 2])
        else:
            tot = x2[h, m] + (r3[h, 0] + r3[h, 1] + r3[h, 2])
            t2[p, g * 8:(g + 1) * 8, :] = tot

    lane = lax.broadcasted_iota(jnp.int32, (8, 128), 1)
    sub = lax.broadcasted_iota(jnp.int32, (8, 128), 0)

    def mirror_rows(p, g):
        h = p * 4 + g
        moved = []
        for m in range(4):
            val = x2[h, m]
            out = val
            for s in (-3, -2, -1, 1, 2, 3):
                out = jnp.where((lane // 32) - (lane // 8) % 4 == s, pltpu.roll(val, (24 * s) % 128, 1), out)
            moved.append(out)
        for yy in range(4):
            out = moved[yy]
            for m in range(4):
                if m != yy:
                    out = jnp.where(lane // 32 == m, pltpu.roll(moved[m], (32 * (m - yy)) % 128, 1), out)
            ts[p, yy, g * 8:(g + 1) * 8, 0, :] = out

    red = (x, y)
    keep = (y * 8 + z * 2 + c, w)

    def mirror_send(p, bh):
        def one(k, carry):
            e = lax.rem(k + rank, 64)
            dy, dw = e // 16, bh * 16 + lax.rem(e, 16)
            src, dst = ts.at[p, dy, dw], rm.at[p, red[p], keep[p]]
            other = dy * 32 + dw != rank

            @pl.when(other)
            def _():
                pltpu.make_async_remote_copy(
                    src, dst, msend.at[p], mrecv.at[p], device_id=(dy, dw), device_id_type=MESH
                ).start()

            @pl.when(jnp.logical_not(other))
            def _():
                pltpu.make_async_copy(src, dst, mrecv.at[p]).start()

            return carry

        lax.fori_loop(0, 64, one, 0)

    def part(p, bh):
        return ((p, 2 * bh), (p, 2 * bh + 1))

    def first(p, bh):
        core_add(p, bh)
        for q in part(p, bh):
            stage_send(0, *q)

    def second(p, bh):
        for q in part(p, bh):
            stage_recv(0, *q)
            stage_send(1, *q)

    def third(p, bh):
        for q in part(p, bh):
            stage_recv(1, *q)
            stage_send(2, *q)
            mirror_rows(*q)
        mirror_send(p, bh)

    def last(p, bh):
        for q in part(p, bh):
            stage_recv(2, *q)

    for kc in range(3):
        vcopy(0, oc, kc).wait()
        acopy(0, kc).wait()
        unit(0, 0, None, kc * KC, KC, oth, True, kc > 0)
    pl.semaphore_wait(barrier, 10)
    core_copy(0, 0).start()
    core_copy(0, 1).start()
    for kc in range(3):
        vcopy(1, c, kc).wait()
        unit(1, 0, 0, kc * KC, KC, own, False, kc > 0)
    first(0, 0)
    unit(1, 0, 1, 0, K, own, False, False)
    first(0, 1)
    for kc in range(3):
        acopy(1, kc).wait()
    unit(0, 1, 0, 0, K, oth, True, False)
    core_copy(1, 0).start()
    unit(0, 1, 1, 0, K, oth, False, False)
    core_copy(1, 1).start()
    unit(1, 1, 0, 0, K, own, False, False)
    first(1, 0)
    second(0, 0)
    unit(1, 1, 1, 0, K, own, False, False)
    first(1, 1)
    second(0, 1)
    third(0, 0)
    second(1, 0)
    third(0, 1)
    second(1, 1)
    third(1, 0)
    third(1, 1)
    last(0, 0)
    last(0, 1)
    last(1, 0)
    last(1, 1)

    for p in range(2):
        zt[p * 128:(p + 1) * 128, :] = jnp.concatenate([t2[p].T, jnp.zeros((128, 96), jnp.float32)], axis=1)
    dcopy.wait()
    occ_j = jnp.zeros((8, 128), jnp.float32)
    vir_b = jnp.zeros((8, 128), jnp.float32)
    jpos = sub * 4 + lane // 32
    bpos = lane % 32
    for k in range(32):
        occ_j = jnp.where(jpos == k, occ_e[k], occ_j)
        vir_b = jnp.where(bpos == k, vir_e[k], vir_b)
    mine = []
    for i in range(8):
        acc = zt[pl.ds(i * 32, 8, stride=4), :]
        for jj in range(1, 4):
            acc = acc + pltpu.roll(zt[pl.ds(i * 32 + jj, 8, stride=4), :], jj * 32, 1)
        mine.append(drv[i] + acc)

    for p in range(2):
        pltpu.make_async_copy(rm.at[p], rm.at[p], mrecv.at[p]).wait()
        for k in range(32):
            row = (rm[p, 0, k] + rm[p, 1, k]) + (rm[p, 2, k] + rm[p, 3, k])
            for m in range(4):
                at = (k // 2) * 8 + m * 2 + k % 2 if p == 0 else m * 32 + k
                et[at] = row if m == 0 else pltpu.roll(row, 128 - 32 * m, 1)
        tr = et[:, 0, :].T
        for yy in range(4):
            acc = None
            for i in range(4):
                blk = tr[i * 8:(i + 1) * 8, :]
                blk = blk if i == yy else pltpu.roll(blk, (32 * (i - yy)) % 128, 1)
                acc = blk if acc is None else jnp.where(lane // 32 == i, blk, acc)
            t = yy * 2 + p
            wt[t * 8:(t + 1) * 8, :] = acc
    va = vir_e[w]
    for i in range(8):
        tot = mine[i] + wt[pl.ds(i, 8, stride=8), :]
        den = (occ_e[y * 8 + i] + occ_j) - va - vir_b
        out_ref[i] = tot / den

    for p in range(2):
        for bh in range(2):
            core_copy(p, bh).wait_send()
        for g in range(4):
            for s in range(3):
                for cp in stage_copies(s, p, g):
                    cp.wait_send()
    for p in range(2):
        for flat in (rm.at[p, 0:3], rm.at[p, 3, 0:31]):
            pltpu.make_async_copy(flat, flat, msend.at[p]).wait()


def local(amplitudes, ladder_integrals, driver, occ_energy, vir_energy, occ_irrep, vir_tile_irrep):
    f32, bf16 = jnp.float32, jnp.bfloat16
    dma = pltpu.SemaphoreType.DMA
    any_ = pl.BlockSpec(memory_space=pl.ANY)
    smem = pl.BlockSpec(memory_space=pltpu.SMEM)
    out = pl.pallas_call(
        kernel,
        out_shape=jax.ShapeDtypeStruct((8, 8, 128), f32),
        in_specs=[any_, any_, any_, smem, smem, smem, smem],
        out_specs=pl.BlockSpec(memory_space=pltpu.VMEM),
        scratch_shapes=[
            pltpu.VMEM((2, 16, 32, K), bf16),
            pltpu.VMEM((2, 4, 4, 32, K), bf16),
            pltpu.VMEM((8, K), jnp.int32),
            pltpu.VMEM((2, 4, 4, 4, 4, 8, 128), f32),
            pltpu.VMEM((2, 4, 4, 4, 4, 8, 128), f32),
            pltpu.VMEM((2, 4, 4, 4, 4, 8, 128), f32),
            pltpu.VMEM((8, 3, 4, 4, 8, 128), f32),
            pltpu.VMEM((8, 4, 4, 8, 128), f32),
            pltpu.VMEM((8, 3, 4, 8, 128), f32),
            pltpu.VMEM((8, 4, 8, 128), f32),
            pltpu.VMEM((8, 3, 8, 128), f32),
            pltpu.VMEM((2, 32, 128), f32),
            pltpu.VMEM((2, 4, 32, 1, 128), f32),
            pltpu.VMEM((2, 4, 32, 1, 128), f32),
            pltpu.VMEM((128, 1, 128), f32),
            pltpu.VMEM((256, 128), f32),
            pltpu.VMEM((64, 128), f32),
            pltpu.VMEM((8, 8, 128), f32),
            dma((2, 3)), dma((2, 3)), dma,
            dma((4,)), dma((4,)),
            dma((8, 3)), dma((8, 3)), dma((8, 3)), dma((8, 3)), dma((8, 3)), dma((8, 3)),
            dma((2,)), dma((2,)),
        ],
        compiler_params=pltpu.CompilerParams(
            collective_id=0, has_side_effects=True, vmem_limit_bytes=60 * 2**20
        ),
        name="ladder",
    )(
        ladder_integrals.reshape(16, 2, 32, K),
        amplitudes.reshape(4, 2, 4, 32, K),
        driver.reshape(8, 8, 128),
        occ_energy, vir_energy, occ_irrep, vir_tile_irrep,
    )
    return out.reshape(8, 1, 1024)


def solution(mesh):
    return jax.shard_map(
        local,
        mesh=mesh,
        in_specs=(
            P(None, None, ("occ", "vir")),
            P(None, None, ("occ", "vir")),
            P("occ", "vir", None),
            P(),
            P(),
            P(),
            P(),
        ),
        out_specs=P("occ", "vir", None),
        check_vma=False,
    )
```

```python
import jax
import jax.numpy as jnp
from jax import lax
from jax.experimental import pallas as pl
from jax.experimental.pallas import tpu as pltpu
from jax.sharding import PartitionSpec as P

NV = 768
TILE = 64
K = 4608
KC = 1536
MESH = pl.DeviceIdType.MESH

ORDERS = ("yzx", "zyx", "yzx", "yzx", "xzy", "xzy", "zxy", "xzy")


def kernel(
    v_hbm, a_hbm, drv_hbm, occ_e, vir_e, occ_l, tile_l, out_ref,
    v, a, lab, own, oth, rc, r1, x1, r2, x2, r3, t2, ts, rm, et, zt, wt, drv,
    vsem, asem, dsem, csend, crecv, s1, q1, s2, q2, s3, q3, msend, mrecv,
):
    y = lax.axis_index("occ")
    w = lax.axis_index("vir")
    z, x, c = w // 8, (w // 2) % 4, w % 2
    oc = 1 - c
    me = {"y": y, "z": z, "x": x}

    def peer(axis, r):
        m = lax.rem(me[axis] + r, 4)
        if axis == "y":
            return m, (m, w)
        if axis == "z":
            return m, (y, m * 8 + x * 2 + c)
        return m, (y, z * 8 + m * 2 + c)

    partner = (y, z * 8 + x * 2 + oc)
    barrier = pltpu.get_barrier_semaphore()
    pl.semaphore_signal(barrier, inc=1, device_id=partner, device_id_type=MESH)
    for axis in "yzx":
        for r in (1, 2, 3):
            pl.semaphore_signal(barrier, inc=1, device_id=peer(axis, r)[1], device_id_type=MESH)

    def vcopy(half, core, kc):
        ks = pl.ds(kc * KC, KC)
        return pltpu.make_async_copy(v_hbm.at[:, core, :, ks], v.at[half, :, :, ks], vsem.at[half, kc])

    def acopy(p, kc):
        ks = pl.ds(kc * KC, KC)
        return pltpu.make_async_copy(a_hbm.at[:, p, :, :, ks], a.at[p, :, :, :, ks], asem.at[p, kc])

    for kc in range(3):
        vcopy(0, oc, kc).start()
        acopy(0, kc).start()
    for kc in range(3):
        vcopy(1, c, kc).start()
    for kc in range(3):
        acopy(1, kc).start()
    dcopy = pltpu.make_async_copy(drv_hbm, drv, dsem)
    dcopy.start()

    d_pos = lax.broadcasted_iota(jnp.int32, (8, NV), 1) // TILE
    d_lab = jnp.zeros((8, NV), jnp.int32)
    for t in range(NV // TILE):
        d_lab = jnp.where(d_pos == t, tile_l[t], d_lab)
    rank = y * 32 + w
    for cl in range(K // NV):
        c_lab = tile_l[(rank * (K // NV) + cl) // TILE]
        lab[:, pl.ds(cl * NV, NV)] = jnp.bitwise_xor(d_lab, c_lab)
    row = lax.broadcasted_iota(jnp.int32, (32, 128), 0)
    occ_col = jnp.zeros((32, 128), jnp.int32)
    for j in range(32):
        occ_col = jnp.where(row == j, occ_l[j], occ_col)
    occ_col = occ_col[:, :1].astype(jnp.float32).astype(jnp.bfloat16)

    def masked(p, k0, kt):
        parts = []
        base = lab[0:1, pl.ds(k0, kt)]
        for yy in range(4):
            for i in range(4):
                want = jnp.bitwise_xor(base, occ_l[yy * 8 + p * 4 + i])
                want = want.astype(jnp.float32).astype(jnp.bfloat16)
                blk = a[p, yy, i, :, pl.ds(k0, kt)]
                blk = jnp.where(occ_col == want, blk, jnp.zeros_like(blk))
                a[p, yy, i, :, pl.ds(k0, kt)] = blk
                parts.append(blk)
        return jnp.concatenate(parts, axis=0)

    def unit(half, p, bh, k0, kt, dst, first, add):
        lo, n = (0, 32) if bh is None else (bh * 16, 16)
        rhs = masked(p, k0, kt) if first else a[p, :, :, :, pl.ds(k0, kt)].reshape(512, kt)
        lhs = v[half, :, lo:lo + n, pl.ds(k0, kt)].reshape(16 * n, kt)
        d = lax.dot_general(lhs, rhs, (((1,), (1,)), ((), ())), preferred_element_type=jnp.float32)
        gs = slice(lo // 8, (lo + n) // 8)
        for yy in range(4):
            blk = d[:, yy * 128:(yy + 1) * 128].reshape(4, 4, n // 8, 8, 128)
            if add:
                dst[p, yy, :, :, gs] += blk
            else:
                dst[p, yy, :, :, gs] = blk

    def core_copy(p, bh):
        gs = pl.ds(2 * bh, 2)
        return pltpu.make_async_remote_copy(
            oth.at[p, :, :, :, gs], rc.at[p, :, :, :, gs], csend.at[2 * p + bh], crecv.at[2 * p + bh],
            device_id=partner, device_id_type=MESH,
        )

    def core_add(p, bh):
        core_copy(p, bh).wait_recv()
        gs = pl.ds(2 * bh, 2)
        own[p, :, :, :, gs] = own[p, :, :, :, gs] + rc[p, :, :, :, gs]

    def at_axis(ref, lead, names, axis, m):
        idx = tuple(lead) + tuple(m if n == axis else slice(None) for n in names)
        return ref.at[idx]

    def stage_copies(s, p, g):
        h = p * 4 + g
        order = ORDERS[h]
        axis = order[s]
        out = []
        for r in (1, 2, 3):
            m, dev = peer(axis, r)
            if s == 0:
                src = own.at[tuple([p] + [m if n == axis else slice(None) for n in "yzx"] + [g])]
                dst, ss, rs = r1.at[h, r - 1], s1.at[h, r - 1], q1.at[h, r - 1]
            elif s == 1:
                names = [n for n in "yzx" if n != order[0]]
                src = x1.at[tuple([h] + [m if n == axis else slice(None) for n in names])]
                dst, ss, rs = r2.at[h, r - 1], s2.at[h, r - 1], q2.at[h, r - 1]
            else:
                src = x2.at[h, m]
                dst, ss, rs = r3.at[h, r - 1], s3.at[h, r - 1], q3.at[h, r - 1]
            out.append(pltpu.make_async_remote_copy(src, dst, ss, rs, device_id=dev, device_id_type=MESH))
        return out

    def stage_send(s, p, g):
        for cp in stage_copies(s, p, g):
            cp.start()

    def stage_recv(s, p, g):
        h = p * 4 + g
        order = ORDERS[h]
        axis = order[s]
        m = me[axis]
        for cp in stage_copies(s, p, g):
            cp.wait_recv()
        if s == 0:
            mine = own[tuple([p] + [m if n == axis else slice(None) for n in "yzx"] + [g])]
            x1[h] = mine + (r1[h, 0] + r1[h, 1] + r1[h, 2])
        elif s == 1:
            names = [n for n in "yzx" if n != order[0]]
            mine = x1[tuple([h] + [m if n == axis else slice(None) for n in names])]
            x2[h] = mine + (r2[h, 0] + r2[h, 1] + r2[h, 2])
        else:
            tot = x2[h, m] + (r3[h, 0] + r3[h, 1] + r3[h, 2])
            t2[p, g * 8:(g + 1) * 8, :] = tot

    lane = lax.broadcasted_iota(jnp.int32, (8, 128), 1)
    sub = lax.broadcasted_iota(jnp.int32, (8, 128), 0)

    def mirror_rows(p, g):
        h = p * 4 + g
        moved = []
        for m in range(4):
            val = x2[h, m]
            out = val
            for s in (-3, -2, -1, 1, 2, 3):
                out = jnp.where((lane // 32) - (lane // 8) % 4 == s, pltpu.roll(val, (24 * s) % 128, 1), out)
            moved.append(out)
        for yy in range(4):
            out = moved[yy]
            for m in range(4):
                if m != yy:
                    out = jnp.where(lane // 32 == m, pltpu.roll(moved[m], (32 * (m - yy)) % 128, 1), out)
            ts[p, yy, g * 8:(g + 1) * 8, 0, :] = out

    red = (x, y)
    keep = (y * 8 + z * 2 + c, w)

    def mirror_send(p, bh):
        def one(k, carry):
            e = lax.rem(k + rank, 64)
            dy, dw = e // 16, bh * 16 + lax.rem(e, 16)
            src, dst = ts.at[p, dy, dw], rm.at[p, red[p], keep[p]]
            other = dy * 32 + dw != rank

            @pl.when(other)
            def _():
                pltpu.make_async_remote_copy(
                    src, dst, msend.at[p], mrecv.at[p], device_id=(dy, dw), device_id_type=MESH
                ).start()

            @pl.when(jnp.logical_not(other))
            def _():
                pltpu.make_async_copy(src, dst, mrecv.at[p]).start()

            return carry

        lax.fori_loop(0, 64, one, 0)

    def part(p, bh):
        return ((p, 2 * bh), (p, 2 * bh + 1))

    def first(p, bh):
        core_add(p, bh)
        for q in part(p, bh):
            stage_send(0, *q)

    def second(p, bh):
        for q in part(p, bh):
            stage_recv(0, *q)
            stage_send(1, *q)

    def third(p, bh):
        for q in part(p, bh):
            stage_recv(1, *q)
            stage_send(2, *q)
            mirror_rows(*q)
        mirror_send(p, bh)

    def last(p, bh):
        for q in part(p, bh):
            stage_recv(2, *q)

    for kc in range(3):
        vcopy(0, oc, kc).wait()
        acopy(0, kc).wait()
        unit(0, 0, None, kc * KC, KC, oth, True, kc > 0)
    pl.semaphore_wait(barrier, 10)
    core_copy(0, 0).start()
    core_copy(0, 1).start()
    for kc in range(3):
        vcopy(1, c, kc).wait()
        unit(1, 0, 0, kc * KC, KC, own, False, kc > 0)
    first(0, 0)
    unit(1, 0, 1, 0, K, own, False, False)
    first(0, 1)
    for kc in range(3):
        acopy(1, kc).wait()
    unit(0, 1, 0, 0, K, oth, True, False)
    core_copy(1, 0).start()
    unit(0, 1, 1, 0, K, oth, False, False)
    core_copy(1, 1).start()
    unit(1, 1, 0, 0, K, own, False, False)
    first(1, 0)
    second(0, 0)
    unit(1, 1, 1, 0, K, own, False, False)
    first(1, 1)
    second(0, 1)
    third(0, 0)
    second(1, 0)
    second(1, 1)
    third(0, 1)
    third(1, 0)
    third(1, 1)
    last(0, 0)
    last(0, 1)
    last(1, 0)
    last(1, 1)

    for p in range(2):
        zt[p * 128:(p + 1) * 128, :] = jnp.concatenate([t2[p].T, jnp.zeros((128, 96), jnp.float32)], axis=1)
    dcopy.wait()
    occ_j = jnp.zeros((8, 128), jnp.float32)
    vir_b = jnp.zeros((8, 128), jnp.float32)
    jpos = sub * 4 + lane // 32
    bpos = lane % 32
    for k in range(32):
        occ_j = jnp.where(jpos == k, occ_e[k], occ_j)
        vir_b = jnp.where(bpos == k, vir_e[k], vir_b)
    mine = []
    for i in range(8):
        acc = zt[pl.ds(i * 32, 8, stride=4), :]
        for jj in range(1, 4):
            acc = acc + pltpu.roll(zt[pl.ds(i * 32 + jj, 8, stride=4), :], jj * 32, 1)
        mine.append(drv[i] + acc)

    for p in range(2):
        pltpu.make_async_copy(rm.at[p], rm.at[p], mrecv.at[p]).wait()
        for k in range(32):
            row = (rm[p, 0, k] + rm[p, 1, k]) + (rm[p, 2, k] + rm[p, 3, k])
            for m in range(4):
                at = (k // 2) * 8 + m * 2 + k % 2 if p == 0 else m * 32 + k
                et[at] = row if m == 0 else pltpu.roll(row, 128 - 32 * m, 1)
        tr = et[:, 0, :].T
        for yy in range(4):
            acc = None
            for i in range(4):
                blk = tr[i * 8:(i + 1) * 8, :]
                blk = blk if i == yy else pltpu.roll(blk, (32 * (i - yy)) % 128, 1)
                acc = blk if acc is None else jnp.where(lane // 32 == i, blk, acc)
            t = yy * 2 + p
            wt[t * 8:(t + 1) * 8, :] = acc
    va = vir_e[w]
    for i in range(8):
        tot = mine[i] + wt[pl.ds(i, 8, stride=8), :]
        den = (occ_e[y * 8 + i] + occ_j) - va - vir_b
        out_ref[i] = tot / den

    for p in range(2):
        for bh in range(2):
            core_copy(p, bh).wait_send()
        for g in range(4):
            for s in range(3):
                for cp in stage_copies(s, p, g):
                    cp.wait_send()
    for p in range(2):
        for flat in (rm.at[p, 0:3], rm.at[p, 3, 0:31]):
            pltpu.make_async_copy(flat, flat, msend.at[p]).wait()


def local(amplitudes, ladder_integrals, driver, occ_energy, vir_energy, occ_irrep, vir_tile_irrep):
    f32, bf16 = jnp.float32, jnp.bfloat16
    dma = pltpu.SemaphoreType.DMA
    any_ = pl.BlockSpec(memory_space=pl.ANY)
    smem = pl.BlockSpec(memory_space=pltpu.SMEM)
    out = pl.pallas_call(
        kernel,
        out_shape=jax.ShapeDtypeStruct((8, 8, 128), f32),
        in_specs=[any_, any_, any_, smem, smem, smem, smem],
        out_specs=pl.BlockSpec(memory_space=pltpu.VMEM),
        scratch_shapes=[
            pltpu.VMEM((2, 16, 32, K), bf16),
            pltpu.VMEM((2, 4, 4, 32, K), bf16),
            pltpu.VMEM((8, K), jnp.int32),
            pltpu.VMEM((2, 4, 4, 4, 4, 8, 128), f32),
            pltpu.VMEM((2, 4, 4, 4, 4, 8, 128), f32),
            pltpu.VMEM((2, 4, 4, 4, 4, 8, 128), f32),
            pltpu.VMEM((8, 3, 4, 4, 8, 128), f32),
            pltpu.VMEM((8, 4, 4, 8, 128), f32),
            pltpu.VMEM((8, 3, 4, 8, 128), f32),
            pltpu.VMEM((8, 4, 8, 128), f32),
            pltpu.VMEM((8, 3, 8, 128), f32),
            pltpu.VMEM((2, 32, 128), f32),
            pltpu.VMEM((2, 4, 32, 1, 128), f32),
            pltpu.VMEM((2, 4, 32, 1, 128), f32),
            pltpu.VMEM((128, 1, 128), f32),
            pltpu.VMEM((256, 128), f32),
            pltpu.VMEM((64, 128), f32),
            pltpu.VMEM((8, 8, 128), f32),
            dma((2, 3)), dma((2, 3)), dma,
            dma((4,)), dma((4,)),
            dma((8, 3)), dma((8, 3)), dma((8, 3)), dma((8, 3)), dma((8, 3)), dma((8, 3)),
            dma((2,)), dma((2,)),
        ],
        compiler_params=pltpu.CompilerParams(
            collective_id=0, has_side_effects=True, vmem_limit_bytes=60 * 2**20
        ),
        name="ladder",
    )(
        ladder_integrals.reshape(16, 2, 32, K),
        amplitudes.reshape(4, 2, 4, 32, K),
        driver.reshape(8, 8, 128),
        occ_energy, vir_energy, occ_irrep, vir_tile_irrep,
    )
    return out.reshape(8, 1, 1024)


def solution(mesh):
    return jax.shard_map(
        local,
        mesh=mesh,
        in_specs=(
            P(None, None, ("occ", "vir")),
            P(None, None, ("occ", "vir")),
            P("occ", "vir", None),
            P(),
            P(),
            P(),
            P(),
        ),
        out_specs=P("occ", "vir", None),
        check_vma=False,
    )
```
